256 devices in a mesh: seq: 64 (over x, z_hi, y), heads: 4 (over z_lo, core).
Axes of the slice: x: 4, y: 4, z: 8 (z_hi: 4, z_lo: 2; z = z_hi * 2 + z_lo), core: 2. Of those that a mesh axis runs over, the one named last changes fastest.
Arguments:
- queries: bfloat16 [131072, 2048], P('seq', 'heads'), may hold values from -120 to 120
- keys: bfloat16 [512, 2048], P(None, 'heads'), may hold values from -4.2 to 4.2
- values: bfloat16 [512, 2048], P(None, 'heads'), may hold values from -6 to 6
- out_grad: bfloat16 [131072, 2048], P('seq', 'heads'), may hold values from -6 to 6
- key_proj: bfloat16 [2048, 2048], P(None, 'heads'), may hold values from -0.125 to 0.125
- value_proj: bfloat16 [2048, 2048], P(None, 'heads'), may hold values from -0.125 to 0.125
- global_in: bfloat16 [512, 2048], P('seq', 'heads'), may hold values from -6 to 6
- up_proj: bfloat16 [2048, 8192], P('heads', 'seq'), may hold values from -0.125 to 0.125
- down_proj: bfloat16 [8192, 2048], P('seq', 'heads'), may hold values from -0.0625 to 0.0625
Outputs:
- query_grad: bfloat16 [131072, 2048], P('seq', 'heads')
- global_grad: float32 [512, 2048], P('seq', 'heads')
The draws below stay inside these ranges and needn't reach their ends.
All inputs are finite; a program needn't handle non-finite values.
Results may differ from the reference program's by a relative error of at most 0.014.
Values may be sent and summed in bfloat16 or wider, within the bound.
A program may use at most 128 MiB of HBM per device.

```python
import jax
import jax.numpy as jnp
from jax import lax

H = 16
HD = 128
D = 2048
F = 8192
G = 512
TOKENS = 131072


def base_keys(key):
    raw = jnp.clip(jax.random.normal(jax.random.fold_in(key, 7), (G, D), jnp.float32), -4.0, 4.0)
    return raw


def draw_keys(key, part):
    return base_keys(key).astype(jnp.bfloat16)


def draw_queries(key, part):
    raw = jnp.clip(jax.random.normal(jax.random.fold_in(key, 5), (TOKENS, D), jnp.float32), -4.0, 4.0)
    return raw.astype(jnp.bfloat16)


def steps_of(stream_key, dims, split, smallest, largest):
    level, own = 1.0, jax.random.fold_in(stream_key, 6)
    for axis_at, shards_of in split:
        heights = jnp.exp(jax.random.uniform(jax.random.fold_in(own, axis_at), (shards_of,), jnp.float32, smallest / len(split), largest / len(split)))
        level = level * jnp.repeat(heights, dims[axis_at] // shards_of).reshape([-1 if axis == axis_at else 1 for axis in range(len(dims))])
    return level


def centred(own_key, dims, spread, reach, split=(), held_as=jnp.bfloat16):
    level = steps_of(own_key, dims, split, -0.22, 0.18) if split else 1.0
    values = jax.random.normal(own_key, dims, jnp.float32) * spread * level
    return jnp.minimum(jnp.maximum(values, -reach), reach).astype(held_as)


def setup_inputs(seed: int = 0) -> dict:
    key_of = jax.random.split(jax.random.key(seed), 10)
    queries = draw_queries(jax.random.fold_in(key_of[9], 71), 0)
    keys = draw_keys(jax.random.fold_in(key_of[9], 71), 0)
    values = centred(key_of[2], (G, D), 1.0, 6.0, ((1, 4),))
    out_grad = centred(key_of[3], (TOKENS, D), 1.0, 6.0, ((0, 64), (1, 4)))
    key_proj = centred(key_of[4], (D, D), D ** -0.5, 0.125, ((1, 4),))
    value_proj = centred(key_of[5], (D, D), D ** -0.5, 0.125, ((1, 4),))
    global_in = centred(key_of[6], (G, D), 1.0, 6.0, ((0, 64), (1, 4)))
    up_proj = centred(key_of[7], (D, F), D ** -0.5, 0.125, ((0, 4), (1, 64)))
    down_proj = centred(key_of[8], (F, D), F ** -0.5, 0.0625, ((0, 64), (1, 4)))
    return {"queries": queries, "keys": keys, "values": values, "out_grad": out_grad, "key_proj": key_proj, "value_proj": value_proj, "global_in": global_in, "up_proj": up_proj, "down_proj": down_proj}


def slope_of(pre):
    return 0.5 * (1.0 + lax.erf(pre * 0.7071067811865476)) + pre * jnp.exp(-0.5 * pre * pre) * 0.3989422804014327


def reference(queries, keys, values, out_grad, key_proj, value_proj, global_in, up_proj, down_proj):
    scale = HD ** -0.5
    tok_count = queries.shape[0]
    query_heads = queries.reshape(tok_count, H, HD).transpose(1, 0, 2)
    grad_heads = out_grad.reshape(tok_count, H, HD).transpose(1, 0, 2)
    key_heads = keys.reshape(G, H, HD).transpose(1, 0, 2)
    value_heads = values.reshape(G, H, HD).transpose(1, 0, 2)

    def one_head(inputs):
        query_one, key_one, value_one, grad_one = inputs
        scores = scale * jnp.dot(query_one, key_one.T, preferred_element_type=jnp.float32)
        weights = jax.nn.softmax(scores, axis=-1)
        weight_grad = jnp.dot(grad_one, value_one.T, preferred_element_type=jnp.float32)
        centre = jnp.sum(weights * weight_grad, axis=-1, keepdims=True)
        score_grad = (weights * (weight_grad - centre)).astype(jnp.bfloat16)
        weights_low = weights.astype(jnp.bfloat16)
        query_part = (scale * jnp.dot(score_grad, key_one, preferred_element_type=jnp.float32)).astype(jnp.bfloat16)
        key_part = scale * jnp.dot(score_grad.T, query_one, preferred_element_type=jnp.float32)
        value_part = jnp.dot(weights_low.T, grad_one, preferred_element_type=jnp.float32)
        return query_part, key_part, value_part

    query_parts, key_parts, value_parts = lax.map(one_head, (query_heads, key_heads, value_heads, grad_heads))
    query_grad = query_parts.transpose(1, 0, 2).reshape(tok_count, D)
    key_low = key_parts.transpose(1, 0, 2).reshape(G, D).astype(jnp.bfloat16)
    value_low = value_parts.transpose(1, 0, 2).reshape(G, D).astype(jnp.bfloat16)
    state_grad = jnp.dot(key_low, key_proj.T, preferred_element_type=jnp.float32) + jnp.dot(value_low, value_proj.T, preferred_element_type=jnp.float32)
    state_low = state_grad.astype(jnp.bfloat16)
    pre = jnp.dot(global_in, up_proj, preferred_element_type=jnp.float32)
    back = jnp.dot(state_low, down_proj.T, preferred_element_type=jnp.float32)
    gated = (slope_of(pre) * back).astype(jnp.bfloat16)
    global_grad = state_grad + jnp.dot(gated, up_proj.T, preferred_element_type=jnp.float32)
    return query_grad, global_grad
```

```python
import functools

import jax
import jax.numpy as jnp
from jax import lax
from jax.experimental import pallas as pl
from jax.experimental.pallas import tpu as pltpu
from jax.sharding import PartitionSpec as P

HD = 128
ROWS = 8
SCALE = HD ** (-0.5)
SCALE_LOG2E = SCALE * 1.4426950408889634
NT = (((1,), (1,)), ((), ()))
MESH = pl.DeviceIdType.MESH
F32 = jnp.float32
BF16 = jnp.bfloat16


def slope_of(pre):
    return (
        0.5 * (1.0 + lax.erf(pre * 0.7071067811865476))
        + pre * jnp.exp(-0.5 * pre * pre) * 0.3989422804014327
    )


def grid_of(seq):
    return {64: (4, 4, 4), 4: (2, 2, 1)}[seq]


def kernel(
    dims,
    q_hbm, k_hbm, v_hbm, g_hbm, kp_hbm, vp_hbm, gin_hbm, up_hbm, down_hbm,
    dq_hbm, gg_hbm,
    q, g, k, v, dq, wcat, up, down, gin,
    a1_send, a1_recv, state, a2_send, a2_recv, c_all,
    pre32, p_send, p_recv, slope, back32, d_send, d_recv, gated,
    e32, e_send, e_recv, gg,
    in_sem, w_sem, misc_sem, out_sem,
    wsend_sem, wrecv_sem, gsend_sem, grecv_sem,
    a1s_sem, a1r_sem, a2s_sem, a2r_sem, cs_sem, cr_sem,
    ps_sem, pr_sem, ds_sem, dr_sem, es_sem, er_sem,
):
    nx, nz, ny, nh = dims
    planes = nx * ny
    local_heads = q.shape[0]
    width = local_heads * HD
    half = planes * ROWS // 2
    hid = down_hbm.shape[0]
    s = lax.axis_index("seq")
    h = lax.axis_index("heads")
    x, z, y = s // (nz * ny), (s // ny) % nz, s % ny
    core = h % 2
    xy = x * ny + y
    zh = z * nh + h

    def seq_of(ax, az, ay):
        return (ax * nz + az) * ny + ay

    plane_peers = []
    for dx in range(nx):
        for dy in range(ny):
            if dx or dy:
                px, py = (x + dx) % nx, (y + dy) % ny
                plane_peers.append((px * ny + py, {"seq": seq_of(px, z, py), "heads": h}))
    column_peers = []
    for dz in range(nz):
        for dh in range(nh):
            if dz or dh:
                pz, ph = (z + dz) % nz, (h + dh) % nh
                column_peers.append((pz * nh + ph, {"seq": seq_of(x, pz, y), "heads": ph}))
    depth_peers = [{"seq": seq_of(x, (z + dz) % nz, y), "heads": h} for dz in range(1, nz)]
    partner = {"seq": s, "heads": h + 1 - 2 * core}
    across = {"seq": s, "heads": (h + 2) % nh}

    def remote(src, dst, send_sem, recv_sem, peer):
        return pltpu.make_async_remote_copy(
            src_ref=src, dst_ref=dst, send_sem=send_sem, recv_sem=recv_sem,
            device_id=peer, device_id_type=MESH,
        )

    def await_recv(ref, sem):
        pltpu.make_async_copy(ref, ref, sem).wait()

    barrier = pltpu.get_barrier_semaphore()
    for _, peer in plane_peers + column_peers:
        pl.semaphore_signal(barrier, inc=1, device_id=peer, device_id_type=MESH)

    loads = []
    for i in range(local_heads):
        cols = pl.ds(i * HD, HD)
        loads.append([
            pltpu.make_async_copy(src.at[:, cols], dst.at[i], in_sem.at[i, n])
            for n, (src, dst) in enumerate(((k_hbm, k), (q_hbm, q), (v_hbm, v), (g_hbm, g)))
        ])
    own_up = pltpu.make_async_copy(up_hbm, up.at[:, pl.ds(0, hid)], misc_sem.at[0])
    own_down = pltpu.make_async_copy(down_hbm, down.at[pl.ds(0, hid), :], misc_sem.at[1])
    own_gin = pltpu.make_async_copy(gin_hbm, gin.at[xy], misc_sem.at[2])
    for copy in loads[0]:
        copy.start()
    own_up.start()
    own_down.start()
    own_gin.start()
    for group in loads[1:]:
        for copy in group:
            copy.start()
    weight_loads = []
    for i in range(local_heads):
        cols = pl.ds(i * HD, HD)
        for n, src in enumerate((kp_hbm, vp_hbm)):
            weight_loads.append(
                pltpu.make_async_copy(src.at[:, cols], wcat.at[i, :, pl.ds(n * HD, HD)], w_sem.at[i, n])
            )
            weight_loads[-1].start()

    def attend(i):
        for copy in loads[i]:
            copy.wait()
        q_i, g_i, k_i, v_i = q[i], g[i], k[i], v[i]
        scores = lax.dot_general(k_i, q_i, NT, preferred_element_type=F32)
        weight_grad = lax.dot_general(v_i, g_i, NT, preferred_element_type=F32)
        top = jnp.max(scores, axis=0, keepdims=True)
        e = jnp.exp2((scores - top) * SCALE_LOG2E)
        inv = 1.0 / jnp.sum(e, axis=0, keepdims=True)
        weights = e * inv
        centre = jnp.sum(e * weight_grad, axis=0, keepdims=True) * inv
        score_grad = (weights * (weight_grad - centre)).astype(BF16)
        weights_low = weights.astype(BF16)
        query_grad = jnp.dot(k_i.T, score_grad, preferred_element_type=F32) * SCALE
        dq[i] = query_grad.astype(BF16).T
        dk = jnp.dot(score_grad, q_i, preferred_element_type=F32) * SCALE
        dv = jnp.dot(weights_low, g_i, preferred_element_type=F32)
        for ax in range(nx):
            for az in range(nz):
                for ay in range(ny):
                    r = seq_of(ax, az, ay) * ROWS
                    a1_send[i, ax * ny + ay, az] = jnp.concatenate(
                        [dk[r:r + ROWS], dv[r:r + ROWS]], axis=0
                    ).astype(BF16)

    def out_copy(i):
        return pltpu.make_async_copy(dq.at[i], dq_hbm.at[:, pl.ds(i * HD, HD)], out_sem.at[i])

    def a1_copies(i):
        return [
            remote(a1_send.at[i, pxy], a1_recv.at[i, n], a1s_sem.at[i], a1r_sem.at[i], peer)
            for n, (pxy, peer) in enumerate(plane_peers)
        ]

    def launch(i):
        out_copy(i).start()
        for copy in a1_copies(i):
            copy.start()

    def project(i):
        weight_loads[2 * i].wait()
        weight_loads[2 * i + 1].wait()
        await_recv(a1_recv.at[i], a1r_sem.at[i])
        total = a1_send[i, xy].astype(F32)
        for n in range(planes - 1):
            total = total + a1_recv[i, n].astype(F32)
        low = jnp.concatenate(
            [total[:, :ROWS].reshape(nz * ROWS, HD), total[:, ROWS:].reshape(nz * ROWS, HD)], axis=1
        ).astype(BF16)
        return lax.dot_general(low, wcat[i], NT, preferred_element_type=F32)

    attend(0)

    pl.semaphore_wait(barrier, len(plane_peers) + len(column_peers))
    own_gin.wait()
    gin_copies = [
        remote(gin.at[xy], gin.at[xy], gsend_sem, grecv_sem, peer) for _, peer in plane_peers
    ]
    own_up.wait()
    own_down.wait()
    weight_copies = []
    for n, peer in enumerate(depth_peers):
        span = pl.ds((n + 1) * hid, hid)
        weight_copies.append(
            remote(up.at[:, pl.ds(0, hid)], up.at[:, span], wsend_sem.at[0], wrecv_sem.at[0], peer)
        )
        weight_copies.append(
            remote(down.at[pl.ds(0, hid), :], down.at[span, :], wsend_sem.at[1], wrecv_sem.at[1], peer)
        )
    for copy in gin_copies + weight_copies:
        copy.start()
    launch(0)

    for i in range(1, local_heads):
        attend(i)
        launch(i)
        part = project(i - 1)
        state[...] = part if i == 1 else state[...] + part

    await_recv(gin.at[pl.ds(0, planes - 1)], grecv_sem)
    await_recv(up.at[:, pl.ds(hid, (nz - 1) * hid)], wrecv_sem.at[0])
    rows_in = gin[...].astype(F32).reshape(planes * ROWS, width).astype(BF16)
    pre = jnp.dot(rows_in, up[...], preferred_element_type=F32)
    pre32[0] = pre[:half]
    pre32[1] = pre[half:]
    p_send[0] = pre32[1 - core].astype(BF16)
    p_first = remote(p_send.at[0], p_recv.at[0], ps_sem.at[0], pr_sem.at[0], partner)
    p_first.start()
    p_first.wait_recv()
    pre_half = pre32[core] + p_recv[0].astype(F32)
    p_send[1] = pre_half.astype(BF16)
    p_second = remote(p_send.at[1], p_recv.at[1], ps_sem.at[1], pr_sem.at[1], across)
    p_second.start()
    p_second.wait_recv()
    slope[...] = slope_of(pre_half + p_recv[1].astype(F32))

    total = state[...] + project(local_heads - 1)
    for az in range(nz):
        for ah in range(nh):
            piece = total[az * ROWS:(az + 1) * ROWS, ah * width:(ah + 1) * width]
            a2_send[az * nh + ah] = piece.astype(BF16)
    a2_copies = [
        remote(a2_send.at[pzh], a2_recv.at[n], a2s_sem, a2r_sem, peer)
        for n, (pzh, peer) in enumerate(column_peers)
    ]
    for copy in a2_copies:
        copy.start()
    await_recv(a2_recv, a2r_sem)
    own_state = a2_send[zh].astype(F32)
    for n in range(nz * nh - 1):
        own_state = own_state + a2_recv[n].astype(F32)

    c_all[xy] = own_state.astype(BF16)
    c_copies = [remote(c_all.at[xy], c_all.at[xy], cs_sem, cr_sem, peer) for _, peer in plane_peers]
    for copy in c_copies:
        copy.start()
    await_recv(down.at[pl.ds(hid, (nz - 1) * hid), :], wrecv_sem.at[1])
    await_recv(c_all.at[pl.ds(0, planes - 1)], cr_sem)
    rows_state = c_all[...].astype(F32).reshape(planes * ROWS, width).astype(BF16)
    back = lax.dot_general(rows_state, down[...], NT, preferred_element_type=F32)
    back32[0] = back[:half]
    back32[1] = back[half:]
    d_send[0] = back32[1 - core].astype(BF16)
    d_first = remote(d_send.at[0], d_recv.at[0], ds_sem.at[0], dr_sem.at[0], partner)
    d_first.start()
    d_first.wait_recv()
    back_half = back32[core] + d_recv[0].astype(F32)
    d_send[1] = back_half.astype(BF16)
    d_second = remote(d_send.at[1], d_recv.at[1], ds_sem.at[1], dr_sem.at[1], across)
    d_second.start()
    d_second.wait_recv()
    gated[core] = (slope[...] * (back_half + d_recv[1].astype(F32))).astype(BF16)
    d_third = remote(gated.at[core], gated.at[core], ds_sem.at[2], dr_sem.at[2], partner)
    d_third.start()
    d_third.wait_recv()

    full = jnp.concatenate([gated[0], gated[1]], axis=0)
    out = lax.dot_general(full, up[...], NT, preferred_element_type=F32)
    out = out.reshape(planes, ROWS, width)
    e32[...] = out
    e_send[...] = out.astype(BF16)
    e_copies = [
        remote(e_send.at[pxy], e_recv.at[n], es_sem, er_sem, peer)
        for n, (pxy, peer) in enumerate(plane_peers)
    ]
    for copy in e_copies:
        copy.start()
    await_recv(e_recv, er_sem)
    result = own_state + e32[xy]
    for n in range(planes - 1):
        result = result + e_recv[n].astype(F32)
    gg[...] = result
    last = pltpu.make_async_copy(gg, gg_hbm, misc_sem.at[3])
    last.start()

    for i in range(local_heads):
        out_copy(i).wait()
        await_recv(a1_recv.at[i], a1s_sem.at[i])
    await_recv(gin.at[pl.ds(0, planes - 1)], gsend_sem)
    await_recv(up.at[:, pl.ds(hid, (nz - 1) * hid)], wsend_sem.at[0])
    await_recv(down.at[pl.ds(hid, (nz - 1) * hid), :], wsend_sem.at[1])
    p_first.wait_send()
    p_second.wait_send()
    await_recv(a2_recv, a2s_sem)
    await_recv(c_all.at[pl.ds(0, planes - 1)], cs_sem)
    d_first.wait_send()
    d_second.wait_send()
    d_third.wait_send()
    await_recv(e_recv, es_sem)
    last.wait()


def local(queries, keys, values, out_grad, key_proj, value_proj, global_in, up_proj, down_proj):
    seq, nh = lax.axis_size("seq"), lax.axis_size("heads")
    nx, nz, ny = grid_of(seq)
    planes = nx * ny
    tokens, width = queries.shape
    globs = keys.shape[0]
    heads = width // HD
    model = key_proj.shape[0]
    hid = down_proj.shape[0]
    half = planes * ROWS // 2
    all_hid = nz * hid
    dma, vmem = pltpu.SemaphoreType.DMA, pltpu.VMEM
    anywhere = pl.BlockSpec(memory_space=pl.ANY)
    return pl.pallas_call(
        functools.partial(kernel, (nx, nz, ny, nh)),
        out_shape=(
            jax.ShapeDtypeStruct((tokens, width), BF16),
            jax.ShapeDtypeStruct((ROWS, width), F32),
        ),
        in_specs=[anywhere] * 9,
        out_specs=(anywhere, anywhere),
        scratch_shapes=[
            vmem((heads, tokens, HD), BF16),
            vmem((heads, tokens, HD), BF16),
            vmem((heads, globs, HD), BF16),
            vmem((heads, globs, HD), BF16),
            vmem((heads, tokens, HD), BF16),
            vmem((heads, model, 2 * HD), BF16),
            vmem((width, all_hid), BF16),
            vmem((all_hid, width), BF16),
            vmem((planes, ROWS, width), BF16),
            vmem((heads, planes, nz, 2 * ROWS, HD), BF16),
            vmem((heads, planes - 1, nz, 2 * ROWS, HD), BF16),
            vmem((nz * ROWS, model), F32),
            vmem((nz * nh, ROWS, width), BF16),
            vmem((nz * nh - 1, ROWS, width), BF16),
            vmem((planes, ROWS, width), BF16),
            vmem((2, half, all_hid), F32),
            vmem((2, half, all_hid), BF16),
            vmem((2, half, all_hid), BF16),
            vmem((half, all_hid), F32),
            vmem((2, half, all_hid), F32),
            vmem((2, half, all_hid), BF16),
            vmem((2, half, all_hid), BF16),
            vmem((2, half, all_hid), BF16),
            vmem((planes, ROWS, width), F32),
            vmem((planes, ROWS, width), BF16),
            vmem((planes - 1, ROWS, width), BF16),
            vmem((ROWS, width), F32),
            dma((heads, 4)), dma((heads, 2)), dma((4,)), dma((heads,)),
            dma((2,)), dma((2,)), dma, dma,
            dma((heads,)), dma((heads,)), dma, dma, dma, dma,
            dma((2,)), dma((2,)), dma((3,)), dma((3,)), dma, dma,
        ],
        compiler_params=pltpu.CompilerParams(
            collective_id=0, has_side_effects=True, vmem_limit_bytes=60 * 1024 * 1024
        ),
    )(queries, keys, values, out_grad, key_proj, value_proj, global_in, up_proj, down_proj)


def solution(mesh):
    placed = (
        P("seq", "heads"),
        P(None, "heads"),
        P(None, "heads"),
        P("seq", "heads"),
        P(None, "heads"),
        P(None, "heads"),
        P("seq", "heads"),
        P("heads", "seq"),
        P("seq", "heads"),
    )
    return jax.shard_map(
        local,
        mesh=mesh,
        in_specs=placed,
        out_specs=(P("seq", "heads"), P("seq", "heads")),
        check_vma=False,
    )
```

```python
import functools

import jax
import jax.numpy as jnp
from jax import lax
from jax.experimental import pallas as pl
from jax.experimental.pallas import tpu as pltpu
from jax.sharding import PartitionSpec as P

HD = 128
ROWS = 8
SCALE = HD ** (-0.5)
SCALE_LOG2E = SCALE * 1.4426950408889634
NT = (((1,), (1,)), ((), ()))
MESH = pl.DeviceIdType.MESH
F32 = jnp.float32
BF16 = jnp.bfloat16


def slope_of(pre):
    return (
        0.5 * (1.0 + lax.erf(pre * 0.7071067811865476))
        + pre * jnp.exp(-0.5 * pre * pre) * 0.3989422804014327
    )


def grid_of(seq):
    return {64: (4, 4, 4), 4: (2, 2, 1)}[seq]


def kernel(
    dims,
    q_hbm, k_hbm, v_hbm, g_hbm, kp_hbm, vp_hbm, gin_hbm, up_hbm, down_hbm,
    dq, gg,
    q, g, k, v, sg, wl, wcat, up, down, gin,
    a1_send, a1_recv, state, a2_send, a2_recv, c_all,
    pre32, p_send, p_recv, slope, back32, d_send, d_recv, gated,
    e32, e_send, e_recv,
    in_sem, w_sem, misc_sem,
    wsend_sem, wrecv_sem, gsend_sem, grecv_sem,
    a1s_sem, a1r_sem, a2s_sem, a2r_sem, cs_sem, cr_sem,
    ps_sem, pr_sem, ds_sem, dr_sem, es_sem, er_sem,
):
    nx, nz, ny, nh = dims
    planes = nx * ny
    local_heads, tokens = q.shape[:2]
    chunk = min(512, tokens)
    width = local_heads * HD
    half = planes * ROWS // 2
    hid = down_hbm.shape[0]
    s = lax.axis_index("seq")
    h = lax.axis_index("heads")
    x, z, y = s // (nz * ny), (s // ny) % nz, s % ny
    core = h % 2
    xy = x * ny + y
    zh = z * nh + h

    def seq_of(ax, az, ay):
        return (ax * nz + az) * ny + ay

    plane_peers = []
    for dx in range(nx):
        for dy in range(ny):
            if dx or dy:
                px, py = (x + dx) % nx, (y + dy) % ny
                plane_peers.append((px * ny + py, {"seq": seq_of(px, z, py), "heads": h}))
    column_peers = []
    for dz in range(nz):
        for dh in range(nh):
            if dz or dh:
                pz, ph = (z + dz) % nz, (h + dh) % nh
                column_peers.append((pz * nh + ph, {"seq": seq_of(x, pz, y), "heads": ph}))
    depth_peers = [{"seq": seq_of(x, (z + dz) % nz, y), "heads": h} for dz in range(1, nz)]
    partner = {"seq": s, "heads": h + 1 - 2 * core}
    across = {"seq": s, "heads": (h + 2) % nh}

    def remote(src, dst, send_sem, recv_sem, peer):
        return pltpu.make_async_remote_copy(
            src_ref=src, dst_ref=dst, send_sem=send_sem, recv_sem=recv_sem,
            device_id=peer, device_id_type=MESH,
        )

    def await_recv(ref, sem):
        pltpu.make_async_copy(ref, ref, sem).wait()

    barrier = pltpu.get_barrier_semaphore()
    for _, peer in plane_peers + column_peers:
        pl.semaphore_signal(barrier, inc=1, device_id=peer, device_id_type=MESH)

    loads = []
    for i in range(local_heads):
        cols = pl.ds(i * HD, HD)
        loads.append([
            pltpu.make_async_copy(src.at[:, cols], dst.at[i], in_sem.at[i, n])
            for n, (src, dst) in enumerate(((k_hbm, k), (q_hbm, q), (v_hbm, v), (g_hbm, g)))
        ])
    own_up = pltpu.make_async_copy(up_hbm, up.at[:, pl.ds(0, hid)], misc_sem.at[0])
    own_down = pltpu.make_async_copy(down_hbm, down.at[pl.ds(0, hid), :], misc_sem.at[1])
    own_gin = pltpu.make_async_copy(gin_hbm, gin.at[xy], misc_sem.at[2])
    for copy in loads[0]:
        copy.start()
    own_up.start()
    own_down.start()
    own_gin.start()
    for group in loads[1:]:
        for copy in group:
            copy.start()
    weight_loads = []
    for i in range(local_heads):
        cols = pl.ds(i * HD, HD)
        for n, src in enumerate((kp_hbm, vp_hbm)):
            weight_loads.append(
                pltpu.make_async_copy(src.at[:, cols], wcat.at[i, :, pl.ds(n * HD, HD)], w_sem.at[i, n])
            )
            weight_loads[-1].start()

    def attend(i):
        for copy in loads[i]:
            copy.wait()
        k_i, v_i = k[i], v[i]
        for start in range(0, tokens, chunk):
            part = slice(start, start + chunk)
            scores = lax.dot_general(k_i, q[i, part], NT, preferred_element_type=F32)
            weight_grad = lax.dot_general(v_i, g[i, part], NT, preferred_element_type=F32)
            top = jnp.max(scores, axis=0, keepdims=True)
            e = jnp.exp2((scores - top) * SCALE_LOG2E)
            inv = 1.0 / jnp.sum(e, axis=0, keepdims=True)
            weights = e * inv
            centre = jnp.sum(e * weight_grad, axis=0, keepdims=True) * inv
            sg[i, :, part] = (weights * (weight_grad - centre)).astype(BF16)
            wl[:, part] = weights.astype(BF16)
        dv = jnp.dot(wl[...], g[i], preferred_element_type=F32)
        dk = jnp.dot(sg[i], q[i], preferred_element_type=F32) * SCALE
        for ax in range(nx):
            for az in range(nz):
                for ay in range(ny):
                    r = seq_of(ax, az, ay) * ROWS
                    a1_send[i, ax * ny + ay, az] = jnp.concatenate(
                        [dk[r:r + ROWS], dv[r:r + ROWS]], axis=0
                    ).astype(BF16)

    def query_part(i):
        query_grad = jnp.dot(k[i].T, sg[i], preferred_element_type=F32) * SCALE
        dq[:, i * HD:(i + 1) * HD] = query_grad.astype(BF16).T

    def a1_copies(i):
        return [
            remote(a1_send.at[i, pxy], a1_recv.at[i, n], a1s_sem.at[i], a1r_sem.at[i], peer)
            for n, (pxy, peer) in enumerate(plane_peers)
        ]

    def launch(i):
        for copy in a1_copies(i):
            copy.start()

    def project(i):
        weight_loads[2 * i].wait()
        weight_loads[2 * i + 1].wait()
        await_recv(a1_recv.at[i], a1r_sem.at[i])
        total = a1_send[i, xy].astype(F32)
        for n in range(planes - 1):
            total = total + a1_recv[i, n].astype(F32)
        low = jnp.concatenate(
            [total[:, :ROWS].reshape(nz * ROWS, HD), total[:, ROWS:].reshape(nz * ROWS, HD)], axis=1
        ).astype(BF16)
        return lax.dot_general(low, wcat[i], NT, preferred_element_type=F32)

    attend(0)

    pl.semaphore_wait(barrier, len(plane_peers) + len(column_peers))
    own_gin.wait()
    gin_copies = [
        remote(gin.at[xy], gin.at[xy], gsend_sem, grecv_sem, peer) for _, peer in plane_peers
    ]
    own_up.wait()
    own_down.wait()
    up_copies, down_copies = [], []
    for n, peer in enumerate(depth_peers):
        span = pl.ds((n + 1) * hid, hid)
        up_copies.append(
            remote(up.at[:, pl.ds(0, hid)], up.at[:, span], wsend_sem.at[0], wrecv_sem.at[0], peer)
        )
        down_copies.append(
            remote(down.at[pl.ds(0, hid), :], down.at[span, :], wsend_sem.at[1], wrecv_sem.at[1], peer)
        )
    for copy in up_copies + gin_copies:
        copy.start()
    launch(0)

    for i in range(1, local_heads):
        attend(i)
        launch(i)
        if i == 1:
            for copy in down_copies:
                copy.start()
        part = project(i - 1)
        state[...] = part if i == 1 else state[...] + part

    await_recv(gin.at[pl.ds(0, planes - 1)], grecv_sem)
    await_recv(up.at[:, pl.ds(hid, (nz - 1) * hid)], wrecv_sem.at[0])
    rows_in = gin[...].astype(F32).reshape(planes * ROWS, width).astype(BF16)
    pre = jnp.dot(rows_in, up[...], preferred_element_type=F32)
    pre32[0] = pre[:half]
    pre32[1] = pre[half:]
    p_send[0] = pre32[1 - core].astype(BF16)
    p_first = remote(p_send.at[0], p_recv.at[0], ps_sem.at[0], pr_sem.at[0], partner)
    p_first.start()
    query_part(0)
    p_first.wait_recv()
    pre_half = pre32[core] + p_recv[0].astype(F32)
    p_send[1] = pre_half.astype(BF16)
    p_second = remote(p_send.at[1], p_recv.at[1], ps_sem.at[1], pr_sem.at[1], across)
    p_second.start()
    query_part(1)
    query_part(2)
    p_second.wait_recv()
    slope[...] = slope_of(pre_half + p_recv[1].astype(F32))
    query_part(3)

    total = state[...] + project(local_heads - 1)
    for az in range(nz):
        for ah in range(nh):
            piece = total[az * ROWS:(az + 1) * ROWS, ah * width:(ah + 1) * width]
            a2_send[az * nh + ah] = piece.astype(BF16)
    a2_copies = [
        remote(a2_send.at[pzh], a2_recv.at[n], a2s_sem, a2r_sem, peer)
        for n, (pzh, peer) in enumerate(column_peers)
    ]
    for copy in a2_copies:
        copy.start()
    await_recv(a2_recv, a2r_sem)
    own_state = a2_send[zh].astype(F32)
    for n in range(nz * nh - 1):
        own_state = own_state + a2_recv[n].astype(F32)

    c_all[xy] = own_state.astype(BF16)
    c_copies = [remote(c_all.at[xy], c_all.at[xy], cs_sem, cr_sem, peer) for _, peer in plane_peers]
    for copy in c_copies:
        copy.start()
    await_recv(down.at[pl.ds(hid, (nz - 1) * hid), :], wrecv_sem.at[1])
    await_recv(c_all.at[pl.ds(0, planes - 1)], cr_sem)
    rows_state = c_all[...].astype(F32).reshape(planes * ROWS, width).astype(BF16)
    back = lax.dot_general(rows_state, down[...], NT, preferred_element_type=F32)
    back32[0] = back[:half]
    back32[1] = back[half:]
    d_send[0] = back32[1 - core].astype(BF16)
    d_first = remote(d_send.at[0], d_recv.at[0], ds_sem.at[0], dr_sem.at[0], partner)
    d_first.start()
    d_first.wait_recv()
    back_half = back32[core] + d_recv[0].astype(F32)
    d_send[1] = back_half.astype(BF16)
    d_second = remote(d_send.at[1], d_recv.at[1], ds_sem.at[1], dr_sem.at[1], across)
    d_second.start()
    d_second.wait_recv()
    gated[core] = (slope[...] * (back_half + d_recv[1].astype(F32))).astype(BF16)
    d_third = remote(gated.at[core], gated.at[core], ds_sem.at[2], dr_sem.at[2], partner)
    d_third.start()
    d_third.wait_recv()

    full = jnp.concatenate([gated[0], gated[1]], axis=0)
    out = lax.dot_general(full, up[...], NT, preferred_element_type=F32)
    out = out.reshape(planes, ROWS, width)
    e32[...] = out
    e_send[...] = out.astype(BF16)
    e_copies = [
        remote(e_send.at[pxy], e_recv.at[n], es_sem, er_sem, peer)
        for n, (pxy, peer) in enumerate(plane_peers)
    ]
    for copy in e_copies:
        copy.start()
    await_recv(e_recv, er_sem)
    result = own_state + e32[xy]
    for n in range(planes - 1):
        result = result + e_recv[n].astype(F32)
    gg[...] = result

    for i in range(local_heads):
        await_recv(a1_recv.at[i], a1s_sem.at[i])
    await_recv(gin.at[pl.ds(0, planes - 1)], gsend_sem)
    await_recv(up.at[:, pl.ds(hid, (nz - 1) * hid)], wsend_sem.at[0])
    await_recv(down.at[pl.ds(hid, (nz - 1) * hid), :], wsend_sem.at[1])
    p_first.wait_send()
    p_second.wait_send()
    await_recv(a2_recv, a2s_sem)
    await_recv(c_all.at[pl.ds(0, planes - 1)], cs_sem)
    d_first.wait_send()
    d_second.wait_send()
    d_third.wait_send()
    await_recv(e_recv, es_sem)


def local(queries, keys, values, out_grad, key_proj, value_proj, global_in, up_proj, down_proj):
    seq, nh = lax.axis_size("seq"), lax.axis_size("heads")
    nx, nz, ny = grid_of(seq)
    planes = nx * ny
    tokens, width = queries.shape
    globs = keys.shape[0]
    heads = width // HD
    model = key_proj.shape[0]
    hid = down_proj.shape[0]
    half = planes * ROWS // 2
    all_hid = nz * hid
    dma, vmem = pltpu.SemaphoreType.DMA, pltpu.VMEM
    anywhere = pl.BlockSpec(memory_space=pl.ANY)
    return pl.pallas_call(
        functools.partial(kernel, (nx, nz, ny, nh)),
        out_shape=(
            pltpu.VMEM((tokens, width), BF16),
            pltpu.VMEM((ROWS, width), F32),
        ),
        in_specs=[anywhere] * 9,
        out_specs=(pl.BlockSpec(memory_space=pltpu.VMEM),) * 2,
        scratch_shapes=[
            vmem((heads, tokens, HD), BF16),
            vmem((heads, tokens, HD), BF16),
            vmem((heads, globs, HD), BF16),
            vmem((heads, globs, HD), BF16),
            vmem((heads, globs, tokens), BF16),
            vmem((globs, tokens), BF16),
            vmem((heads, model, 2 * HD), BF16),
            vmem((width, all_hid), BF16),
            vmem((all_hid, width), BF16),
            vmem((planes, ROWS, width), BF16),
            vmem((heads, planes, nz, 2 * ROWS, HD), BF16),
            vmem((heads, planes - 1, nz, 2 * ROWS, HD), BF16),
            vmem((nz * ROWS, model), F32),
            vmem((nz * nh, ROWS, width), BF16),
            vmem((nz * nh - 1, ROWS, width), BF16),
            vmem((planes, ROWS, width), BF16),
            vmem((2, half, all_hid), F32),
            vmem((2, half, all_hid), BF16),
            vmem((2, half, all_hid), BF16),
            vmem((half, all_hid), F32),
            vmem((2, half, all_hid), F32),
            vmem((2, half, all_hid), BF16),
            vmem((2, half, all_hid), BF16),
            vmem((2, half, all_hid), BF16),
            vmem((planes, ROWS, width), F32),
            vmem((planes, ROWS, width), BF16),
            vmem((planes - 1, ROWS, width), BF16),
            dma((heads, 4)), dma((heads, 2)), dma((3,)),
            dma((2,)), dma((2,)), dma, dma,
            dma((heads,)), dma((heads,)), dma, dma, dma, dma,
            dma((2,)), dma((2,)), dma((3,)), dma((3,)), dma, dma,
        ],
        compiler_params=pltpu.CompilerParams(
            collective_id=0, has_side_effects=True, vmem_limit_bytes=60000 * 1024,
        ),
    )(queries, keys, values, out_grad, key_proj, value_proj, global_in, up_proj, down_proj)


def solution(mesh):
    placed = (
        P("seq", "heads"),
        P(None, "heads"),
        P(None, "heads"),
        P("seq", "heads"),
        P(None, "heads"),
        P(None, "heads"),
        P("seq", "heads"),
        P("heads", "seq"),
        P("seq", "heads"),
    )
    return jax.shard_map(
        local,
        mesh=mesh,
        in_specs=placed,
        out_specs=(P("seq", "heads"), P("seq", "heads")),
        check_vma=False,
    )
```

```python
import functools

import jax
import jax.numpy as jnp
from jax import lax
from jax.experimental import pallas as pl
from jax.experimental.pallas import tpu as pltpu
from jax.sharding import PartitionSpec as P

HD = 128
ROWS = 8
SCALE = HD ** (-0.5)
SCALE_LOG2E = SCALE * 1.4426950408889634
NT = (((1,), (1,)), ((), ()))
MESH = pl.DeviceIdType.MESH
F32 = jnp.float32
BF16 = jnp.bfloat16


def slope_of(pre):
    return (
        0.5 * (1.0 + lax.erf(pre * 0.7071067811865476))
        + pre * jnp.exp(-0.5 * pre * pre) * 0.3989422804014327
    )


def softmax_grad(q, g, k, v):
    scores = lax.dot_general(k, q, NT, preferred_element_type=F32)
    weight_grad = lax.dot_general(v, g, NT, preferred_element_type=F32)
    top = jnp.max(scores, axis=0, keepdims=True)
    e = jnp.exp2((scores - top) * SCALE_LOG2E)
    inv = 1.0 / jnp.sum(e, axis=0, keepdims=True)
    centre = jnp.sum(e * weight_grad, axis=0, keepdims=True) * inv
    weights = e * inv
    return weights.astype(BF16), (weights * (weight_grad - centre)).astype(BF16)


def grid_of(seq):
    return {64: (4, 4, 4), 4: (2, 2, 1)}[seq]


def kernel(
    dims,
    q_hbm, k_hbm, v_hbm, g_hbm, kp_hbm, vp_hbm, gin_hbm, up_hbm, down_hbm,
    dq, gg,
    q, g, k, v, sg, wl, wcat, up, down, gin,
    a1_send, a1_recv, state, a2_send, a2_recv, c_all,
    pre32, p_send, p_recv, slope, back32, d_send, d_recv, gated,
    e32, e_send, e_recv,
    in_sem, w_sem, misc_sem,
    wsend_sem, wrecv_sem, gsend_sem, grecv_sem,
    a1s_sem, a1r_sem, a2s_sem, a2r_sem, cs_sem, cr_sem,
    ps_sem, pr_sem, ds_sem, dr_sem, es_sem, er_sem,
):
    nx, nz, ny, nh = dims
    planes = nx * ny
    local_heads, tokens = q.shape[:2]
    chunk = min(2048, tokens)
    width = local_heads * HD
    half = planes * ROWS // 2
    hid = down_hbm.shape[0]
    s = lax.axis_index("seq")
    h = lax.axis_index("heads")
    x, z, y = s // (nz * ny), (s // ny) % nz, s % ny
    core = h % 2
    xy = x * ny + y
    zh = z * nh + h

    def seq_of(ax, az, ay):
        return (ax * nz + az) * ny + ay

    plane_peers = []
    for dx in range(nx):
        for dy in range(ny):
            if dx or dy:
                px, py = (x + dx) % nx, (y + dy) % ny
                plane_peers.append((px * ny + py, {"seq": seq_of(px, z, py), "heads": h}))
    column_peers = []
    for dz in range(nz):
        for dh in range(nh):
            if dz or dh:
                pz, ph = (z + dz) % nz, (h + dh) % nh
                column_peers.append((pz * nh + ph, {"seq": seq_of(x, pz, y), "heads": ph}))
    depth_peers = [{"seq": seq_of(x, (z + dz) % nz, y), "heads": h} for dz in range(1, nz)]
    partner = {"seq": s, "heads": h + 1 - 2 * core}
    across = {"seq": s, "heads": (h + 2) % nh}

    def remote(src, dst, send_sem, recv_sem, peer):
        return pltpu.make_async_remote_copy(
            src_ref=src, dst_ref=dst, send_sem=send_sem, recv_sem=recv_sem,
            device_id=peer, device_id_type=MESH,
        )

    def await_recv(ref, sem):
        pltpu.make_async_copy(ref, ref, sem).wait()

    barrier = pltpu.get_barrier_semaphore()
    for _, peer in plane_peers + column_peers:
        pl.semaphore_signal(barrier, inc=1, device_id=peer, device_id_type=MESH)

    def loads(i):
        cols = pl.ds(pl.multiple_of(i * HD, HD), HD)
        return [
            pltpu.make_async_copy(src.at[:, cols], dst.at[i], in_sem.at[i, n])
            for n, (src, dst) in enumerate(((k_hbm, k), (q_hbm, q), (v_hbm, v), (g_hbm, g)))
        ]

    own_up = pltpu.make_async_copy(up_hbm, up.at[:, pl.ds(0, hid)], misc_sem.at[0])
    own_down = pltpu.make_async_copy(down_hbm, down.at[pl.ds(0, hid), :], misc_sem.at[1])
    own_gin = pltpu.make_async_copy(gin_hbm, gin.at[xy], misc_sem.at[2])
    for copy in loads(0):
        copy.start()
    own_up.start()
    own_down.start()
    own_gin.start()
    for i in range(1, local_heads):
        for copy in loads(i):
            copy.start()
    weight_loads = []
    for i in range(local_heads):
        cols = pl.ds(i * HD, HD)
        for n, src in enumerate((kp_hbm, vp_hbm)):
            weight_loads.append(
                pltpu.make_async_copy(src.at[:, cols], wcat.at[i, :, pl.ds(n * HD, HD)], w_sem.at[i, n])
            )
            weight_loads[-1].start()

    def attend(i):
        for start in range(0, tokens, chunk):
            part = slice(start, start + chunk)
            low, grad = softmax_grad(q[i, part], g[i, part], k[i], v[i])
            wl[:, part] = low
            sg[:, part] = grad
        dv = jnp.dot(wl[...], g[i], preferred_element_type=F32)
        dk = jnp.dot(sg[...], q[i], preferred_element_type=F32) * SCALE
        for ax in range(nx):
            for az in range(nz):
                for ay in range(ny):
                    r = seq_of(ax, az, ay) * ROWS
                    a1_send[i, ax * ny + ay, az] = jnp.concatenate(
                        [dk[r:r + ROWS], dv[r:r + ROWS]], axis=0
                    ).astype(BF16)

    def query_part(i):
        query_grad = jnp.dot(k[i].T, sg[...], preferred_element_type=F32) * SCALE
        dq[:, pl.ds(pl.multiple_of(i * HD, HD), HD)] = query_grad.astype(BF16).T

    def a1_copies(i):
        return [
            remote(a1_send.at[i, pxy], a1_recv.at[i, n], a1s_sem.at[i], a1r_sem.at[i], peer)
            for n, (pxy, peer) in enumerate(plane_peers)
        ]

    def launch(i):
        for copy in a1_copies(i):
            copy.start()

    def project(i):
        weight_loads[2 * i].wait()
        weight_loads[2 * i + 1].wait()
        await_recv(a1_recv.at[i], a1r_sem.at[i])
        total = a1_send[i, xy].astype(F32)
        for n in range(planes - 1):
            total = total + a1_recv[i, n].astype(F32)
        low = jnp.concatenate(
            [total[:, :ROWS].reshape(nz * ROWS, HD), total[:, ROWS:].reshape(nz * ROWS, HD)], axis=1
        ).astype(BF16)
        return lax.dot_general(low, wcat[i], NT, preferred_element_type=F32)

    gin_copies = [
        remote(gin.at[xy], gin.at[xy], gsend_sem, grecv_sem, peer) for _, peer in plane_peers
    ]
    up_copies, down_copies = [], []
    for n, peer in enumerate(depth_peers):
        span = pl.ds((n + 1) * hid, hid)
        up_copies.append(
            remote(up.at[:, pl.ds(0, hid)], up.at[:, span], wsend_sem.at[0], wrecv_sem.at[0], peer)
        )
        down_copies.append(
            remote(down.at[pl.ds(0, hid), :], down.at[span, :], wsend_sem.at[1], wrecv_sem.at[1], peer)
        )
    @pl.loop(0, local_heads)
    def _(i):
        for copy in loads(i):
            copy.wait()
        attend(i)

        @pl.when(i == 0)
        def _():
            own_gin.wait()
            own_up.wait()
            own_down.wait()
            pl.semaphore_wait(barrier, len(plane_peers) + len(column_peers))
            for copy in up_copies + gin_copies:
                copy.start()

        launch(i)

        @pl.when(i == 1)
        def _():
            for copy in down_copies:
                copy.start()

        query_part(i)

    await_recv(gin.at[pl.ds(0, planes - 1)], grecv_sem)
    await_recv(up.at[:, pl.ds(hid, (nz - 1) * hid)], wrecv_sem.at[0])
    rows_in = gin[...].astype(F32).reshape(planes * ROWS, width).astype(BF16)
    pre = jnp.dot(rows_in, up[...], preferred_element_type=F32)
    pre32[0] = pre[:half]
    pre32[1] = pre[half:]
    p_send[0] = pre32[1 - core].astype(BF16)
    p_first = remote(p_send.at[0], p_recv.at[0], ps_sem.at[0], pr_sem.at[0], partner)
    p_first.start()
    state[...] = project(0)
    p_first.wait_recv()
    pre_half = pre32[core] + p_recv[0].astype(F32)
    p_send[1] = pre_half.astype(BF16)
    p_second = remote(p_send.at[1], p_recv.at[1], ps_sem.at[1], pr_sem.at[1], across)
    p_second.start()
    state[...] += project(1)
    state[...] += project(2)
    p_second.wait_recv()
    slope[...] = slope_of(pre_half + p_recv[1].astype(F32))

    total = state[...] + project(local_heads - 1)
    for az in range(nz):
        for ah in range(nh):
            piece = total[az * ROWS:(az + 1) * ROWS, ah * width:(ah + 1) * width]
            a2_send[az * nh + ah] = piece.astype(BF16)
    a2_copies = [
        remote(a2_send.at[pzh], a2_recv.at[n], a2s_sem, a2r_sem, peer)
        for n, (pzh, peer) in enumerate(column_peers)
    ]
    for copy in a2_copies:
        copy.start()
    await_recv(a2_recv, a2r_sem)
    own_state = a2_send[zh].astype(F32)
    for n in range(nz * nh - 1):
        own_state = own_state + a2_recv[n].astype(F32)

    c_all[xy] = own_state.astype(BF16)
    c_copies = [remote(c_all.at[xy], c_all.at[xy], cs_sem, cr_sem, peer) for _, peer in plane_peers]
    for copy in c_copies:
        copy.start()
    await_recv(down.at[pl.ds(hid, (nz - 1) * hid), :], wrecv_sem.at[1])
    await_recv(c_all.at[pl.ds(0, planes - 1)], cr_sem)
    rows_state = c_all[...].astype(F32).reshape(planes * ROWS, width).astype(BF16)
    back = lax.dot_general(rows_state, down[...], NT, preferred_element_type=F32)
    back32[0] = back[:half]
    back32[1] = back[half:]
    d_send[0] = back32[1 - core].astype(BF16)
    d_first = remote(d_send.at[0], d_recv.at[0], ds_sem.at[0], dr_sem.at[0], partner)
    d_first.start()
    d_first.wait_recv()
    back_half = back32[core] + d_recv[0].astype(F32)
    d_send[1] = back_half.astype(BF16)
    d_second = remote(d_send.at[1], d_recv.at[1], ds_sem.at[1], dr_sem.at[1], across)
    d_second.start()
    d_second.wait_recv()
    gated[core] = (slope[...] * (back_half + d_recv[1].astype(F32))).astype(BF16)
    d_third = remote(gated.at[core], gated.at[core], ds_sem.at[2], dr_sem.at[2], partner)
    d_third.start()
    d_third.wait_recv()

    full = jnp.concatenate([gated[0], gated[1]], axis=0)
    out = lax.dot_general(full, up[...], NT, preferred_element_type=F32)
    out = out.reshape(planes, ROWS, width)
    e32[...] = out
    e_send[...] = out.astype(BF16)
    e_copies = [
        remote(e_send.at[pxy], e_recv.at[n], es_sem, er_sem, peer)
        for n, (pxy, peer) in enumerate(plane_peers)
    ]
    for copy in e_copies:
        copy.start()
    await_recv(e_recv, er_sem)
    result = own_state + e32[xy]
    for n in range(planes - 1):
        result = result + e_recv[n].astype(F32)
    gg[...] = result

    for i in range(local_heads):
        await_recv(a1_recv.at[i], a1s_sem.at[i])
    await_recv(gin.at[pl.ds(0, planes - 1)], gsend_sem)
    await_recv(up.at[:, pl.ds(hid, (nz - 1) * hid)], wsend_sem.at[0])
    await_recv(down.at[pl.ds(hid, (nz - 1) * hid), :], wsend_sem.at[1])
    p_first.wait_send()
    p_second.wait_send()
    await_recv(a2_recv, a2s_sem)
    await_recv(c_all.at[pl.ds(0, planes - 1)], cs_sem)
    d_first.wait_send()
    d_second.wait_send()
    d_third.wait_send()
    await_recv(e_recv, es_sem)


def local(queries, keys, values, out_grad, key_proj, value_proj, global_in, up_proj, down_proj):
    seq, nh = lax.axis_size("seq"), lax.axis_size("heads")
    nx, nz, ny = grid_of(seq)
    planes = nx * ny
    tokens, width = queries.shape
    globs = keys.shape[0]
    heads = width // HD
    model = key_proj.shape[0]
    hid = down_proj.shape[0]
    half = planes * ROWS // 2
    all_hid = nz * hid
    dma, vmem = pltpu.SemaphoreType.DMA, pltpu.VMEM
    anywhere = pl.BlockSpec(memory_space=pl.ANY)
    return pl.pallas_call(
        functools.partial(kernel, (nx, nz, ny, nh)),
        out_shape=(
            pltpu.VMEM((tokens, width), BF16),
            pltpu.VMEM((ROWS, width), F32),
        ),
        in_specs=[anywhere] * 9,
        out_specs=(pl.BlockSpec(memory_space=pltpu.VMEM),) * 2,
        scratch_shapes=[
            vmem((heads, tokens, HD), BF16),
            vmem((heads, tokens, HD), BF16),
            vmem((heads, globs, HD), BF16),
            vmem((heads, globs, HD), BF16),
            vmem((globs, tokens), BF16),
            vmem((globs, tokens), BF16),
            vmem((heads, model, 2 * HD), BF16),
            vmem((width, all_hid), BF16),
            vmem((all_hid, width), BF16),
            vmem((planes, ROWS, width), BF16),
            vmem((heads, planes, nz, 2 * ROWS, HD), BF16),
            vmem((heads, planes - 1, nz, 2 * ROWS, HD), BF16),
            vmem((nz * ROWS, model), F32),
            vmem((nz * nh, ROWS, width), BF16),
            vmem((nz * nh - 1, ROWS, width), BF16),
            vmem((planes, ROWS, width), BF16),
            vmem((2, half, all_hid), F32),
            vmem((2, half, all_hid), BF16),
            vmem((2, half, all_hid), BF16),
            vmem((half, all_hid), F32),
            vmem((2, half, all_hid), F32),
            vmem((2, half, all_hid), BF16),
            vmem((2, half, all_hid), BF16),
            vmem((2, half, all_hid), BF16),
            vmem((planes, ROWS, width), F32),
            vmem((planes, ROWS, width), BF16),
            vmem((planes - 1, ROWS, width), BF16),
            dma((heads, 4)), dma((heads, 2)), dma((3,)),
            dma((2,)), dma((2,)), dma, dma,
            dma((heads,)), dma((heads,)), dma, dma, dma, dma,
            dma((2,)), dma((2,)), dma((3,)), dma((3,)), dma, dma,
        ],
        compiler_params=pltpu.CompilerParams(
            collective_id=0, has_side_effects=True, vmem_limit_bytes=60000 * 1024,

        ),
    )(queries, keys, values, out_grad, key_proj, value_proj, global_in, up_proj, down_proj)


def solution(mesh):
    placed = (
        P("seq", "heads"),
        P(None, "heads"),
        P(None, "heads"),
        P("seq", "heads"),
        P(None, "heads"),
        P(None, "heads"),
        P("seq", "heads"),
        P("heads", "seq"),
        P("seq", "heads"),
    )
    return jax.shard_map(
        local,
        mesh=mesh,
        in_specs=placed,
        out_specs=(P("seq", "heads"), P("seq", "heads")),
        check_vma=False,
    )
```

```python
import functools

import jax
import jax.numpy as jnp
from jax import lax
from jax.experimental import pallas as pl
from jax.experimental.pallas import tpu as pltpu
from jax.sharding import PartitionSpec as P

HD = 128
ROWS = 8
SCALE = HD ** (-0.5)
SCALE_LOG2E = SCALE * 1.4426950408889634
NT = (((1,), (1,)), ((), ()))
MESH = pl.DeviceIdType.MESH
F32 = jnp.float32
BF16 = jnp.bfloat16


def slope_of(pre):
    return (
        0.5 * (1.0 + lax.erf(pre * 0.7071067811865476))
        + pre * jnp.exp(-0.5 * pre * pre) * 0.3989422804014327
    )


def softmax_grad(q, g, k, v):
    scores = lax.dot_general(k, q, NT, preferred_element_type=F32)
    weight_grad = lax.dot_general(v, g, NT, preferred_element_type=F32)
    top = jnp.max(scores, axis=0, keepdims=True)
    e = jnp.exp2((scores - top) * SCALE_LOG2E)
    inv = 1.0 / jnp.sum(e, axis=0, keepdims=True)
    centre = jnp.sum(e * weight_grad, axis=0, keepdims=True) * inv
    weights = e * inv
    return weights.astype(BF16), (weights * (weight_grad - centre)).astype(BF16)


def grid_of(seq):
    return {64: (4, 4, 4), 4: (2, 2, 1)}[seq]


def kernel(
    dims,
    q_hbm, k_hbm, v_hbm, g_hbm, kp_hbm, vp_hbm, gin_hbm, up_hbm, down_hbm,
    dq, gg,
    q, g, k, v, sg, wl, wcat, up, down, gin,
    a1_send, a1_recv, state, a2_send, a2_recv, c_all,
    pre32, p_send, p_recv, slope, back32, d_send, d_recv, gated,
    e32, e_send, e_recv,
    in_sem, w_sem, misc_sem,
    wsend_sem, wrecv_sem, gsend_sem, grecv_sem,
    a1s_sem, a1r_sem, a2s_sem, a2r_sem, cs_sem, cr_sem,
    ps_sem, pr_sem, ds_sem, dr_sem, es_sem, er_sem,
):
    nx, nz, ny, nh = dims
    planes = nx * ny
    local_heads, tokens = q.shape[:2]
    chunk = min(512, tokens)
    width = local_heads * HD
    half = planes * ROWS // 2
    hid = down_hbm.shape[0]
    s = lax.axis_index("seq")
    h = lax.axis_index("heads")
    x, z, y = s // (nz * ny), (s // ny) % nz, s % ny
    core = h % 2
    xy = x * ny + y
    zh = z * nh + h

    def seq_of(ax, az, ay):
        return (ax * nz + az) * ny + ay

    plane_peers = []
    for dx in range(nx):
        for dy in range(ny):
            if dx or dy:
                px, py = (x + dx) % nx, (y + dy) % ny
                plane_peers.append((px * ny + py, {"seq": seq_of(px, z, py), "heads": h}))
    column_peers = []
    for dz in range(nz):
        for dh in range(nh):
            if dz or dh:
                pz, ph = (z + dz) % nz, (h + dh) % nh
                column_peers.append((pz * nh + ph, {"seq": seq_of(x, pz, y), "heads": ph}))
    depth_peers = [{"seq": seq_of(x, (z + dz) % nz, y), "heads": h} for dz in range(1, nz)]
    partner = {"seq": s, "heads": h + 1 - 2 * core}
    across = {"seq": s, "heads": (h + 2) % nh}

    def remote(src, dst, send_sem, recv_sem, peer):
        return pltpu.make_async_remote_copy(
            src_ref=src, dst_ref=dst, send_sem=send_sem, recv_sem=recv_sem,
            device_id=peer, device_id_type=MESH,
        )

    def await_recv(ref, sem):
        pltpu.make_async_copy(ref, ref, sem).wait()

    barrier = pltpu.get_barrier_semaphore()
    for _, peer in plane_peers + column_peers:
        pl.semaphore_signal(barrier, inc=1, device_id=peer, device_id_type=MESH)

    def loads(i):
        cols = pl.ds(pl.multiple_of(i * HD, HD), HD)
        return [
            pltpu.make_async_copy(src.at[:, cols], dst.at[i], in_sem.at[i, n])
            for n, (src, dst) in enumerate(((k_hbm, k), (q_hbm, q), (v_hbm, v), (g_hbm, g)))
        ]

    own_up = pltpu.make_async_copy(up_hbm, up.at[:, pl.ds(0, hid)], misc_sem.at[0])
    own_down = pltpu.make_async_copy(down_hbm, down.at[pl.ds(0, hid), :], misc_sem.at[1])
    own_gin = pltpu.make_async_copy(gin_hbm, gin.at[xy], misc_sem.at[2])
    for copy in loads(0):
        copy.start()
    own_up.start()
    own_down.start()
    own_gin.start()
    for i in range(1, local_heads):
        for copy in loads(i):
            copy.start()
    weight_loads = []
    for i in range(local_heads):
        cols = pl.ds(i * HD, HD)
        for n, src in enumerate((kp_hbm, vp_hbm)):
            weight_loads.append(
                pltpu.make_async_copy(src.at[:, cols], wcat.at[i, :, pl.ds(n * HD, HD)], w_sem.at[i, n])
            )
            weight_loads[-1].start()

    def attend(i):
        for start in range(0, tokens, chunk):
            part = slice(start, start + chunk)
            low, grad = softmax_grad(q[i, part], g[i, part], k[i], v[i])
            wl[:, part] = low
            sg[i, :, part] = grad
        dv = jnp.dot(wl[...], g[i], preferred_element_type=F32)
        dk = jnp.dot(sg[i], q[i], preferred_element_type=F32) * SCALE
        for ax in range(nx):
            for az in range(nz):
                for ay in range(ny):
                    r = seq_of(ax, az, ay) * ROWS
                    a1_send[i, ax * ny + ay, az] = jnp.concatenate(
                        [dk[r:r + ROWS], dv[r:r + ROWS]], axis=0
                    ).astype(BF16)

    def query_part(i):
        query_grad = jnp.dot(k[i].T, sg[i], preferred_element_type=F32) * SCALE
        dq[:, pl.ds(pl.multiple_of(i * HD, HD), HD)] = query_grad.astype(BF16).T

    def a1_copies(i):
        return [
            remote(a1_send.at[i, pxy], a1_recv.at[i, n], a1s_sem.at[i], a1r_sem.at[i], peer)
            for n, (pxy, peer) in enumerate(plane_peers)
        ]

    def launch(i):
        for copy in a1_copies(i):
            copy.start()

    def project(i):
        weight_loads[2 * i].wait()
        weight_loads[2 * i + 1].wait()
        await_recv(a1_recv.at[i], a1r_sem.at[i])
        total = a1_send[i, xy].astype(F32)
        for n in range(planes - 1):
            total = total + a1_recv[i, n].astype(F32)
        low = jnp.concatenate(
            [total[:, :ROWS].reshape(nz * ROWS, HD), total[:, ROWS:].reshape(nz * ROWS, HD)], axis=1
        ).astype(BF16)
        return lax.dot_general(low, wcat[i], NT, preferred_element_type=F32)

    gin_copies = [
        remote(gin.at[xy], gin.at[xy], gsend_sem, grecv_sem, peer) for _, peer in plane_peers
    ]
    up_copies, down_copies = [], []
    for n, peer in enumerate(depth_peers):
        span = pl.ds((n + 1) * hid, hid)
        up_copies.append(
            remote(up.at[:, pl.ds(0, hid)], up.at[:, span], wsend_sem.at[0], wrecv_sem.at[0], peer)
        )
        down_copies.append(
            remote(down.at[pl.ds(0, hid), :], down.at[span, :], wsend_sem.at[1], wrecv_sem.at[1], peer)
        )
    @pl.loop(0, local_heads)
    def _(i):
        for copy in loads(i):
            copy.wait()
        attend(i)

        @pl.when(i == 0)
        def _():
            own_gin.wait()
            own_up.wait()
            own_down.wait()
            pl.semaphore_wait(barrier, len(plane_peers) + len(column_peers))
            for copy in up_copies + gin_copies:
                copy.start()

        launch(i)

        @pl.when(i == 1)
        def _():
            for copy in down_copies:
                copy.start()


    @pl.loop(0, local_heads)
    def _(i):
        query_part(i)

    state[...] = project(0)
    for i in range(1, local_heads - 1):
        state[...] += project(i)

    await_recv(gin.at[pl.ds(0, planes - 1)], grecv_sem)
    await_recv(up.at[:, pl.ds(hid, (nz - 1) * hid)], wrecv_sem.at[0])
    rows_in = gin[...].astype(F32).reshape(planes * ROWS, width).astype(BF16)
    pre = jnp.dot(rows_in, up[...], preferred_element_type=F32)
    pre32[0] = pre[:half]
    pre32[1] = pre[half:]
    p_send[0] = pre32[1 - core].astype(BF16)
    p_first = remote(p_send.at[0], p_recv.at[0], ps_sem.at[0], pr_sem.at[0], partner)
    p_first.start()

    total = state[...] + project(local_heads - 1)
    for az in range(nz):
        for ah in range(nh):
            piece = total[az * ROWS:(az + 1) * ROWS, ah * width:(ah + 1) * width]
            a2_send[az * nh + ah] = piece.astype(BF16)
    a2_copies = [
        remote(a2_send.at[pzh], a2_recv.at[n], a2s_sem, a2r_sem, peer)
        for n, (pzh, peer) in enumerate(column_peers)
    ]
    for copy in a2_copies:
        copy.start()
    p_first.wait_recv()
    pre_half = pre32[core] + p_recv[0].astype(F32)
    pre32[core] = pre_half
    p_send[1] = pre_half.astype(BF16)
    p_second = remote(p_send.at[1], p_recv.at[1], ps_sem.at[1], pr_sem.at[1], across)
    p_second.start()
    await_recv(a2_recv, a2r_sem)
    own_state = a2_send[zh].astype(F32)
    for n in range(nz * nh - 1):
        own_state = own_state + a2_recv[n].astype(F32)

    c_all[xy] = own_state.astype(BF16)
    c_copies = [remote(c_all.at[xy], c_all.at[xy], cs_sem, cr_sem, peer) for _, peer in plane_peers]
    for copy in c_copies:
        copy.start()
    p_second.wait_recv()
    slope[...] = slope_of(pre32[core] + p_recv[1].astype(F32))
    await_recv(down.at[pl.ds(hid, (nz - 1) * hid), :], wrecv_sem.at[1])
    await_recv(c_all.at[pl.ds(0, planes - 1)], cr_sem)
    rows_state = c_all[...].astype(F32).reshape(planes * ROWS, width).astype(BF16)
    back = lax.dot_general(rows_state, down[...], NT, preferred_element_type=F32)
    back32[0] = back[:half]
    back32[1] = back[half:]
    d_send[0] = back32[1 - core].astype(BF16)
    d_first = remote(d_send.at[0], d_recv.at[0], ds_sem.at[0], dr_sem.at[0], partner)
    d_first.start()
    d_first.wait_recv()
    back_half = back32[core] + d_recv[0].astype(F32)
    d_send[1] = back_half.astype(BF16)
    d_second = remote(d_send.at[1], d_recv.at[1], ds_sem.at[1], dr_sem.at[1], across)
    d_second.start()
    d_second.wait_recv()
    gated[core] = (slope[...] * (back_half + d_recv[1].astype(F32))).astype(BF16)
    d_third = remote(gated.at[core], gated.at[core], ds_sem.at[2], dr_sem.at[2], partner)
    d_third.start()
    d_third.wait_recv()

    full = jnp.concatenate([gated[0], gated[1]], axis=0)
    out = lax.dot_general(full, up[...], NT, preferred_element_type=F32)
    out = out.reshape(planes, ROWS, width)
    e32[...] = out
    e_send[...] = out.astype(BF16)
    e_copies = [
        remote(e_send.at[pxy], e_recv.at[n], es_sem, er_sem, peer)
        for n, (pxy, peer) in enumerate(plane_peers)
    ]
    for copy in e_copies:
        copy.start()
    await_recv(e_recv, er_sem)
    result = own_state + e32[xy]
    for n in range(planes - 1):
        result = result + e_recv[n].astype(F32)
    gg[...] = result

    for i in range(local_heads):
        await_recv(a1_recv.at[i], a1s_sem.at[i])
    await_recv(gin.at[pl.ds(0, planes - 1)], gsend_sem)
    await_recv(up.at[:, pl.ds(hid, (nz - 1) * hid)], wsend_sem.at[0])
    await_recv(down.at[pl.ds(hid, (nz - 1) * hid), :], wsend_sem.at[1])
    p_first.wait_send()
    p_second.wait_send()
    await_recv(a2_recv, a2s_sem)
    await_recv(c_all.at[pl.ds(0, planes - 1)], cs_sem)
    d_first.wait_send()
    d_second.wait_send()
    d_third.wait_send()
    await_recv(e_recv, es_sem)


def local(queries, keys, values, out_grad, key_proj, value_proj, global_in, up_proj, down_proj):
    seq, nh = lax.axis_size("seq"), lax.axis_size("heads")
    nx, nz, ny = grid_of(seq)
    planes = nx * ny
    tokens, width = queries.shape
    globs = keys.shape[0]
    heads = width // HD
    model = key_proj.shape[0]
    hid = down_proj.shape[0]
    half = planes * ROWS // 2
    all_hid = nz * hid
    dma, vmem = pltpu.SemaphoreType.DMA, pltpu.VMEM
    anywhere = pl.BlockSpec(memory_space=pl.ANY)
    return pl.pallas_call(
        functools.partial(kernel, (nx, nz, ny, nh)),
        out_shape=(
            pltpu.VMEM((tokens, width), BF16),
            pltpu.VMEM((ROWS, width), F32),
        ),
        in_specs=[anywhere] * 9,
        out_specs=(pl.BlockSpec(memory_space=pltpu.VMEM),) * 2,
        scratch_shapes=[
            vmem((heads, tokens, HD), BF16),
            vmem((heads, tokens, HD), BF16),
            vmem((heads, globs, HD), BF16),
            vmem((heads, globs, HD), BF16),
            vmem((heads, globs, tokens), BF16),
            vmem((globs, tokens), BF16),
            vmem((heads, model, 2 * HD), BF16),
            vmem((width, all_hid), BF16),
            vmem((all_hid, width), BF16),
            vmem((planes, ROWS, width), BF16),
            vmem((heads, planes, nz, 2 * ROWS, HD), BF16),
            vmem((heads, planes - 1, nz, 2 * ROWS, HD), BF16),
            vmem((nz * ROWS, model), F32),
            vmem((nz * nh, ROWS, width), BF16),
            vmem((nz * nh - 1, ROWS, width), BF16),
            vmem((planes, ROWS, width), BF16),
            vmem((2, half, all_hid), F32),
            vmem((2, half, all_hid), BF16),
            vmem((2, half, all_hid), BF16),
            vmem((half, all_hid), F32),
            vmem((2, half, all_hid), F32),
            vmem((2, half, all_hid), BF16),
            vmem((2, half, all_hid), BF16),
            vmem((2, half, all_hid), BF16),
            vmem((planes, ROWS, width), F32),
            vmem((planes, ROWS, width), BF16),
            vmem((planes - 1, ROWS, width), BF16),
            dma((heads, 4)), dma((heads, 2)), dma((3,)),
            dma((2,)), dma((2,)), dma, dma,
            dma((heads,)), dma((heads,)), dma, dma, dma, dma,
            dma((2,)), dma((2,)), dma((3,)), dma((3,)), dma, dma,
        ],
        compiler_params=pltpu.CompilerParams(
            collective_id=0, has_side_effects=True, vmem_limit_bytes=60000 * 1024,

        ),
    )(queries, keys, values, out_grad, key_proj, value_proj, global_in, up_proj, down_proj)


def solution(mesh):
    placed = (
        P("seq", "heads"),
        P(None, "heads"),
        P(None, "heads"),
        P("seq", "heads"),
        P(None, "heads"),
        P(None, "heads"),
        P("seq", "heads"),
        P("heads", "seq"),
        P("seq", "heads"),
    )
    return jax.shard_map(
        local,
        mesh=mesh,
        in_specs=placed,
        out_specs=(P("seq", "heads"), P("seq", "heads")),
        check_vma=False,
    )
```

```python
import functools

import jax
import jax.numpy as jnp
from jax import lax
from jax.experimental import pallas as pl
from jax.experimental.pallas import tpu as pltpu
from jax.sharding import PartitionSpec as P

HD = 128
ROWS = 8
SCALE = HD ** (-0.5)
SCALE_LOG2E = SCALE * 1.4426950408889634
NT = (((1,), (1,)), ((), ()))
MESH = pl.DeviceIdType.MESH
F32 = jnp.float32
BF16 = jnp.bfloat16


def slope_of(pre):
    return (
        0.5 * (1.0 + lax.erf(pre * 0.7071067811865476))
        + pre * jnp.exp(-0.5 * pre * pre) * 0.3989422804014327
    )


def softmax_grad(q, g, k, v):
    scores = lax.dot_general(k, q, NT, preferred_element_type=F32)
    weight_grad = lax.dot_general(v, g, NT, preferred_element_type=F32)
    top = jnp.max(scores, axis=0, keepdims=True)
    e = jnp.exp2((scores - top) * SCALE_LOG2E)
    inv = 1.0 / jnp.sum(e, axis=0, keepdims=True)
    centre = jnp.sum(e * weight_grad, axis=0, keepdims=True) * inv
    weights = e * inv
    return weights.astype(BF16), (weights * (weight_grad - centre)).astype(BF16)


def grid_of(seq):
    return {64: (4, 4, 4), 4: (2, 2, 1)}[seq]


def kernel(
    dims,
    q_hbm, k_hbm, v_hbm, g_hbm, kp_hbm, vp_hbm, gin_hbm, up_hbm, down_hbm,
    dq, gg,
    q, g, k, v, sg, wl, wcat, up, down, gin,
    a1_send, a1_recv, state, a2_send, a2_recv, c_all,
    pre32, p_send, p_recv, slope, d_send, d_recv, gated,
    e32, e_send, e_recv,
    in_sem, w_sem, misc_sem,
    wsend_sem, wrecv_sem, gsend_sem, grecv_sem,
    a1s_sem, a1r_sem, a2s_sem, a2r_sem, cs_sem, cr_sem,
    ps_sem, pr_sem, ds_sem, dr_sem, es_sem, er_sem,
):
    nx, nz, ny, nh = dims
    planes = nx * ny
    local_heads, tokens = q.shape[:2]
    chunk = min(512, tokens)
    width = local_heads * HD
    half = planes * ROWS // 2
    hid = down_hbm.shape[0]
    s = lax.axis_index("seq")
    h = lax.axis_index("heads")
    x, z, y = s // (nz * ny), (s // ny) % nz, s % ny
    core = h % 2
    xy = x * ny + y
    zh = z * nh + h

    def seq_of(ax, az, ay):
        return (ax * nz + az) * ny + ay

    plane_peers = []
    for dx in range(nx):
        for dy in range(ny):
            if dx or dy:
                px, py = (x + dx) % nx, (y + dy) % ny
                plane_peers.append((px * ny + py, {"seq": seq_of(px, z, py), "heads": h}))
    column_peers = []
    for dz in range(nz):
        for dh in range(nh):
            if dz or dh:
                pz, ph = (z + dz) % nz, (h + dh) % nh
                column_peers.append((pz * nh + ph, {"seq": seq_of(x, pz, y), "heads": ph}))
    depth_peers = [{"seq": seq_of(x, (z + dz) % nz, y), "heads": h} for dz in range(1, nz)]
    partner = {"seq": s, "heads": h + 1 - 2 * core}
    across = {"seq": s, "heads": (h + 2) % nh}

    def remote(src, dst, send_sem, recv_sem, peer):
        return pltpu.make_async_remote_copy(
            src_ref=src, dst_ref=dst, send_sem=send_sem, recv_sem=recv_sem,
            device_id=peer, device_id_type=MESH,
        )

    def await_recv(ref, sem):
        pltpu.make_async_copy(ref, ref, sem).wait()

    barrier = pltpu.get_barrier_semaphore()
    for _, peer in plane_peers + column_peers:
        pl.semaphore_signal(barrier, inc=1, device_id=peer, device_id_type=MESH)

    def loads(i):
        cols = pl.ds(pl.multiple_of(i * HD, HD), HD)
        return [
            pltpu.make_async_copy(src.at[:, cols], dst.at[i], in_sem.at[i, n])
            for n, (src, dst) in enumerate(((k_hbm, k), (q_hbm, q), (v_hbm, v), (g_hbm, g)))
        ]

    own_up = pltpu.make_async_copy(up_hbm, up.at[:, pl.ds(0, hid)], misc_sem.at[0])
    own_down = pltpu.make_async_copy(down_hbm, down.at[pl.ds(0, hid), :], misc_sem.at[1])
    own_gin = pltpu.make_async_copy(gin_hbm, gin.at[xy], misc_sem.at[2])
    for copy in loads(0):
        copy.start()
    own_up.start()
    own_down.start()
    own_gin.start()
    for i in range(1, local_heads):
        for copy in loads(i):
            copy.start()
    weight_loads = []
    for i in range(local_heads):
        cols = pl.ds(i * HD, HD)
        for n, src in enumerate((kp_hbm, vp_hbm)):
            weight_loads.append(
                pltpu.make_async_copy(src.at[:, cols], wcat.at[i, :, pl.ds(n * HD, HD)], w_sem.at[i, n])
            )
            weight_loads[-1].start()

    def attend(i):
        for start in range(0, tokens, chunk):
            part = slice(start, start + chunk)
            low, grad = softmax_grad(q[i, part], g[i, part], k[i], v[i])
            wl[:, part] = low
            sg[i, :, part] = grad
        dv = jnp.dot(wl[...], g[i], preferred_element_type=F32)
        dk = jnp.dot(sg[i], q[i], preferred_element_type=F32) * SCALE
        for ax in range(nx):
            for az in range(nz):
                for ay in range(ny):
                    r = seq_of(ax, az, ay) * ROWS
                    a1_send[i, ax * ny + ay, az] = jnp.concatenate(
                        [dk[r:r + ROWS], dv[r:r + ROWS]], axis=0
                    ).astype(BF16)

    def query_part(i):
        query_grad = jnp.dot(k[i].T, sg[i], preferred_element_type=F32) * SCALE
        dq[:, pl.ds(pl.multiple_of(i * HD, HD), HD)] = query_grad.astype(BF16).T

    def a1_copies(i):
        return [
            remote(a1_send.at[i, pxy], a1_recv.at[i, n], a1s_sem.at[i], a1r_sem.at[i], peer)
            for n, (pxy, peer) in enumerate(plane_peers)
        ]

    def launch(i):
        for copy in a1_copies(i):
            copy.start()

    def project(i):
        weight_loads[2 * i].wait()
        weight_loads[2 * i + 1].wait()
        await_recv(a1_recv.at[i], a1r_sem.at[i])
        total = a1_send[i, xy].astype(F32)
        for n in range(planes - 1):
            total = total + a1_recv[i, n].astype(F32)
        low = jnp.concatenate(
            [total[:, :ROWS].reshape(nz * ROWS, HD), total[:, ROWS:].reshape(nz * ROWS, HD)], axis=1
        ).astype(BF16)
        return lax.dot_general(low, wcat[i], NT, preferred_element_type=F32)

    gin_copies = [
        remote(gin.at[xy], gin.at[xy], gsend_sem, grecv_sem, peer) for _, peer in plane_peers
    ]
    up_copies, down_copies = [], []
    for n, peer in enumerate(depth_peers):
        span = pl.ds((n + 1) * hid, hid)
        up_copies.append(
            remote(up.at[:, pl.ds(0, hid)], up.at[:, span], wsend_sem.at[0], wrecv_sem.at[0], peer)
        )
        down_copies.append(
            remote(down.at[pl.ds(0, hid), :], down.at[span, :], wsend_sem.at[1], wrecv_sem.at[1], peer)
        )
    @pl.loop(0, local_heads)
    def _(i):
        for copy in loads(i):
            copy.wait()
        attend(i)

        @pl.when(i == 0)
        def _():
            own_gin.wait()
            own_up.wait()
            own_down.wait()
            pl.semaphore_wait(barrier, len(plane_peers) + len(column_peers))
            for copy in up_copies + gin_copies:
                copy.start()

        launch(i)

        @pl.when(i == 1)
        def _():
            for copy in down_copies:
                copy.start()


    @pl.loop(0, local_heads)
    def _(i):
        query_part(i)

    state[...] = project(0)
    for i in range(1, local_heads - 1):
        state[...] += project(i)

    await_recv(gin.at[pl.ds(0, planes - 1)], grecv_sem)
    await_recv(up.at[:, pl.ds(hid, (nz - 1) * hid)], wrecv_sem.at[0])
    rows_in = gin[...].astype(F32).reshape(planes * ROWS, width).astype(BF16)
    pre = jnp.dot(rows_in, up[...], preferred_element_type=F32)
    pre32[0] = pre[:half]
    pre32[1] = pre[half:]
    p_send[0] = pre32[1 - core].astype(BF16)
    p_first = remote(p_send.at[0], p_recv.at[0], ps_sem.at[0], pr_sem.at[0], partner)
    p_first.start()

    total = state[...] + project(local_heads - 1)
    for az in range(nz):
        for ah in range(nh):
            piece = total[az * ROWS:(az + 1) * ROWS, ah * width:(ah + 1) * width]
            a2_send[az * nh + ah] = piece.astype(BF16)
    a2_copies = [
        remote(a2_send.at[pzh], a2_recv.at[n], a2s_sem, a2r_sem, peer)
        for n, (pzh, peer) in enumerate(column_peers)
    ]
    for copy in a2_copies:
        copy.start()
    p_first.wait_recv()
    pre_half = pre32[core] + p_recv[0].astype(F32)
    pre32[core] = pre_half
    p_send[1] = pre_half.astype(BF16)
    p_second = remote(p_send.at[1], p_recv.at[1], ps_sem.at[1], pr_sem.at[1], across)
    p_second.start()
    await_recv(a2_recv, a2r_sem)
    own_state = a2_send[zh].astype(F32)
    for n in range(nz * nh - 1):
        own_state = own_state + a2_recv[n].astype(F32)

    c_all[xy] = own_state.astype(BF16)
    c_copies = [remote(c_all.at[xy], c_all.at[xy], cs_sem, cr_sem, peer) for _, peer in plane_peers]
    for copy in c_copies:
        copy.start()
    p_second.wait_recv()
    slope[...] = slope_of(pre32[core] + p_recv[1].astype(F32))
    await_recv(down.at[pl.ds(hid, (nz - 1) * hid), :], wrecv_sem.at[1])
    await_recv(c_all.at[pl.ds(0, planes - 1)], cr_sem)

    def back_rows(which):
        rows = c_all[pl.ds(which * (planes // 2), planes // 2)]
        rows = rows.astype(F32).reshape(half, width).astype(BF16)
        return lax.dot_general(rows, down[...], NT, preferred_element_type=F32)

    d_send[0] = back_rows(1 - core).astype(BF16)
    d_first = remote(d_send.at[0], d_recv.at[0], ds_sem.at[0], dr_sem.at[0], partner)
    d_first.start()
    back_own = back_rows(core)
    d_first.wait_recv()
    back_half = back_own + d_recv[0].astype(F32)
    d_send[1] = back_half.astype(BF16)
    d_second = remote(d_send.at[1], d_recv.at[1], ds_sem.at[1], dr_sem.at[1], across)
    d_second.start()
    d_second.wait_recv()
    gated[core] = (slope[...] * (back_half + d_recv[1].astype(F32))).astype(BF16)
    d_third = remote(gated.at[core], gated.at[core], ds_sem.at[2], dr_sem.at[2], partner)
    d_third.start()
    d_third.wait_recv()

    full = jnp.concatenate([gated[0], gated[1]], axis=0)
    out = lax.dot_general(full, up[...], NT, preferred_element_type=F32)
    out = out.reshape(planes, ROWS, width)
    e32[...] = out
    e_send[...] = out.astype(BF16)
    e_copies = [
        remote(e_send.at[pxy], e_recv.at[n], es_sem, er_sem, peer)
        for n, (pxy, peer) in enumerate(plane_peers)
    ]
    for copy in e_copies:
        copy.start()
    await_recv(e_recv, er_sem)
    result = own_state + e32[xy]
    for n in range(planes - 1):
        result = result + e_recv[n].astype(F32)
    gg[...] = result

    for i in range(local_heads):
        await_recv(a1_recv.at[i], a1s_sem.at[i])
    await_recv(gin.at[pl.ds(0, planes - 1)], gsend_sem)
    await_recv(up.at[:, pl.ds(hid, (nz - 1) * hid)], wsend_sem.at[0])
    await_recv(down.at[pl.ds(hid, (nz - 1) * hid), :], wsend_sem.at[1])
    p_first.wait_send()
    p_second.wait_send()
    await_recv(a2_recv, a2s_sem)
    await_recv(c_all.at[pl.ds(0, planes - 1)], cs_sem)
    d_first.wait_send()
    d_second.wait_send()
    d_third.wait_send()
    await_recv(e_recv, es_sem)


def local(queries, keys, values, out_grad, key_proj, value_proj, global_in, up_proj, down_proj):
    seq, nh = lax.axis_size("seq"), lax.axis_size("heads")
    nx, nz, ny = grid_of(seq)
    planes = nx * ny
    tokens, width = queries.shape
    globs = keys.shape[0]
    heads = width // HD
    model = key_proj.shape[0]
    hid = down_proj.shape[0]
    half = planes * ROWS // 2
    all_hid = nz * hid
    dma, vmem = pltpu.SemaphoreType.DMA, pltpu.VMEM
    anywhere = pl.BlockSpec(memory_space=pl.ANY)
    return pl.pallas_call(
        functools.partial(kernel, (nx, nz, ny, nh)),
        out_shape=(
            pltpu.VMEM((tokens, width), BF16),
            pltpu.VMEM((ROWS, width), F32),
        ),
        in_specs=[anywhere] * 9,
        out_specs=(pl.BlockSpec(memory_space=pltpu.VMEM),) * 2,
        scratch_shapes=[
            vmem((heads, tokens, HD), BF16),
            vmem((heads, tokens, HD), BF16),
            vmem((heads, globs, HD), BF16),
            vmem((heads, globs, HD), BF16),
            vmem((heads, globs, tokens), BF16),
            vmem((globs, tokens), BF16),
            vmem((heads, model, 2 * HD), BF16),
            vmem((width, all_hid), BF16),
            vmem((all_hid, width), BF16),
            vmem((planes, ROWS, width), BF16),
            vmem((heads, planes, nz, 2 * ROWS, HD), BF16),
            vmem((heads, planes - 1, nz, 2 * ROWS, HD), BF16),
            vmem((nz * ROWS, model), F32),
            vmem((nz * nh, ROWS, width), BF16),
            vmem((nz * nh - 1, ROWS, width), BF16),
            vmem((planes, ROWS, width), BF16),
            vmem((2, half, all_hid), F32),
            vmem((2, half, all_hid), BF16),
            vmem((2, half, all_hid), BF16),
            vmem((half, all_hid), F32),
            vmem((2, half, all_hid), BF16),
            vmem((2, half, all_hid), BF16),
            vmem((2, half, all_hid), BF16),
            vmem((planes, ROWS, width), F32),
            vmem((planes, ROWS, width), BF16),
            vmem((planes - 1, ROWS, width), BF16),
            dma((heads, 4)), dma((heads, 2)), dma((3,)),
            dma((2,)), dma((2,)), dma, dma,
            dma((heads,)), dma((heads,)), dma, dma, dma, dma,
            dma((2,)), dma((2,)), dma((3,)), dma((3,)), dma, dma,
        ],
        compiler_params=pltpu.CompilerParams(
            collective_id=0, has_side_effects=True, vmem_limit_bytes=60000 * 1024,

        ),
    )(queries, keys, values, out_grad, key_proj, value_proj, global_in, up_proj, down_proj)


def solution(mesh):
    placed = (
        P("seq", "heads"),
        P(None, "heads"),
        P(None, "heads"),
        P("seq", "heads"),
        P(None, "heads"),
        P(None, "heads"),
        P("seq", "heads"),
        P("heads", "seq"),
        P("seq", "heads"),
    )
    return jax.shard_map(
        local,
        mesh=mesh,
        in_specs=placed,
        out_specs=(P("seq", "heads"), P("seq", "heads")),
        check_vma=False,
    )
```
